256 devices in a mesh: dp: 8 (over y, core), seq: 32 (over z, x).
Axes of the slice: x: 4, y: 4, z: 8, core: 2. Of those that a mesh axis runs over, the one named last changes fastest.
Arguments:
- query_rows: bfloat16 [8, 8192, 1536], P('dp', 'seq'), may hold values from -36 to 36, as said below
- key_rows: bfloat16 [8, 8192, 1536], P('dp', 'seq'), may hold values from -6 to 6
- value_rows: bfloat16 [8, 8192, 1536], P('dp', 'seq'), may hold values from -6 to 6
- norm_gain: float32 [1536], replicated, may hold values from 0.1 to 1.9
- grad_output: bfloat16 [8, 8192, 1536], P('dp', 'seq'), may hold values from -6 to 6
Outputs:
- attended: bfloat16 [8, 8192, 1536], P('dp', 'seq')
- grad_query: bfloat16 [8, 8192, 1536], P('dp', 'seq')
- grad_key: bfloat16 [8, 8192, 1536], P('dp', 'seq')
- grad_value: bfloat16 [8, 8192, 1536], P('dp', 'seq')
- grad_gain: float32 [1536], replicated
The draws below stay inside these ranges and needn't reach their ends.
Inputs may be any that keep to these rules, and one draw needn't show every extreme that they name: `query_rows`: query features.
All inputs are finite; a program needn't handle non-finite values.
Results may differ from the reference program's by a relative error of at most 0.0057.
Values sent between devices are 32-bit elements; how exact they have to be, the bound alone decides.
A program may use at most 128 MiB of HBM per device.

```python
import math
import jax
import jax.numpy as jnp
from jax import lax

HEADS = 12
HEAD_DIM = 128
BLOCK = 256
INNER = 1536
SEQS = 8
LENGTH = 8192


def draw_query_rows(key, part):
    base_key, row_key, column_key = jax.random.split(key, 3)
    normal_part = jnp.clip(jax.random.normal(base_key, (SEQS, LENGTH, INNER), jnp.float32), -4.0, 4.0)
    row_scale = jnp.exp(jax.random.uniform(row_key, (SEQS, LENGTH, 1), jnp.float32, math.log(0.3), math.log(3.0)))
    column_scale = jnp.exp(jax.random.uniform(column_key, (1, 1, INNER), jnp.float32, math.log(0.3), math.log(3.0)))
    return (normal_part * row_scale * column_scale).astype(jnp.bfloat16)


def block_levels(stream_key, dims, cuts, low, high):
    level, own = 1.0, jax.random.fold_in(stream_key, 6)
    for axis_at, parts in cuts:
        draws = jnp.exp(jax.random.uniform(jax.random.fold_in(own, axis_at), (parts,), jnp.float32, low / len(cuts), high / len(cuts)))
        level = level * jnp.repeat(draws, dims[axis_at] // parts).reshape([-1 if axis == axis_at else 1 for axis in range(len(dims))])
    return level


def bell_draw(rng, shape, width, limit, cuts=(), dtype=jnp.bfloat16):
    factor_of = block_levels(rng, shape, cuts, -0.22, 0.18) if cuts else 1.0
    entries = jax.random.normal(rng, shape, jnp.float32) * width * factor_of
    return jnp.minimum(jnp.maximum(entries, -limit), limit).astype(dtype)


def setup_inputs(seed: int = 0) -> dict:
    streams_of = jax.random.split(jax.random.key(seed), 6)
    return {
        "query_rows": draw_query_rows(jax.random.fold_in(streams_of[5], 71), 0),
        "key_rows": bell_draw(streams_of[1], (SEQS, LENGTH, INNER), 1.0, 6.0, ((0, 8), (1, 32))),
        "value_rows": bell_draw(streams_of[2], (SEQS, LENGTH, INNER), 1.0, 6.0, ((0, 8), (1, 32))),
        "norm_gain": jnp.clip(1.0 + 0.18 * jax.random.normal(streams_of[3], (INNER,), jnp.float32), 0.1, 1.9),
        "grad_output": bell_draw(streams_of[4], (SEQS, LENGTH, INNER), 1.0, 6.0, ((0, 8), (1, 32))),
    }


norm_eps = 1e-05

def lower_mask(length):
    row_index = lax.broadcasted_iota(jnp.int32, (length, length), 0)
    col_index = lax.broadcasted_iota(jnp.int32, (length, length), 1)
    return row_index >= col_index

def rounded(array):
    return lax.optimization_barrier(array.astype(jnp.bfloat16)).astype(jnp.float32)

def reference(query_rows, key_rows, value_rows, norm_gain, grad_output):
    gain_values = norm_gain.astype(jnp.float32)
    causal = lower_mask(BLOCK)[None]
    blocks = LENGTH // BLOCK

    def to_blocks(array):
        return array.astype(jnp.float32).reshape(blocks, BLOCK, HEADS, HEAD_DIM)

    def one_sequence(inputs):
        query_seq, key_seq, value_seq, grad_seq = inputs
        queries = to_blocks(query_seq)
        key_blocks = to_blocks(key_seq)
        value_blocks = to_blocks(value_seq)
        zero_state = jnp.zeros((HEADS, HEAD_DIM, HEAD_DIM), jnp.float32)

        def forward_step(state, block_inputs):
            query_block, key_block, value_block = block_inputs
            state_round = rounded(state)
            weights = rounded(jnp.where(causal, jnp.einsum('chd,thd->hct', query_block, key_block), 0.0))
            combined = jnp.einsum('chd,hde->che', query_block, state_round) + jnp.einsum('hct,the->che', weights, value_block)
            return (state + jnp.einsum('chd,che->hde', key_block, value_block), (combined, state_round))
        unused, (combined, states) = lax.scan(forward_step, zero_state, (queries, key_blocks, value_blocks))
        combined = combined.reshape(LENGTH, INNER)
        inverse = lax.rsqrt(lax.optimization_barrier(jnp.mean(combined * combined, axis=-1, keepdims=True)) + norm_eps)
        normed = combined * inverse
        attended = (normed * gain_values).astype(jnp.bfloat16)
        upstream = grad_seq.astype(jnp.float32)
        gain_part = lax.optimization_barrier(jnp.sum(upstream * normed, axis=0))
        grad_normed = upstream * gain_values
        grad_combined = rounded(inverse * (grad_normed - normed * lax.optimization_barrier(jnp.mean(grad_normed * normed, axis=-1, keepdims=True))))
        grad_blocks = to_blocks(grad_combined)

        def backward_step(suffix, block_inputs):
            query_block, key_block, value_block, grad_block, state_round = block_inputs
            suffix_round = rounded(suffix)
            weights = rounded(jnp.where(causal, jnp.einsum('chd,thd->hct', query_block, key_block), 0.0))
            grad_weights = rounded(jnp.where(causal, jnp.einsum('che,the->hct', grad_block, value_block), 0.0))
            query_grad = jnp.einsum('che,hde->chd', grad_block, state_round) + jnp.einsum('hct,thd->chd', grad_weights, key_block)
            key_grad = jnp.einsum('che,hde->chd', value_block, suffix_round) + jnp.einsum('hct,chd->thd', grad_weights, query_block)
            value_grad = jnp.einsum('chd,hde->che', key_block, suffix_round) + jnp.einsum('hct,che->the', weights, grad_block)
            new_suffix = suffix + jnp.einsum('chd,che->hde', query_block, grad_block)
            return (new_suffix, (query_grad.astype(jnp.bfloat16), key_grad.astype(jnp.bfloat16), value_grad.astype(jnp.bfloat16)))
        unused_two, (query_grads, key_grads, value_grads) = lax.scan(backward_step, zero_state, (queries, key_blocks, value_blocks, grad_blocks, states), reverse=True)
        return (attended, query_grads.reshape(LENGTH, INNER), key_grads.reshape(LENGTH, INNER), value_grads.reshape(LENGTH, INNER), gain_part)
    attended, grad_query, grad_key, grad_value, gain_parts = lax.map(one_sequence, (query_rows, key_rows, value_rows, grad_output))
    return (attended, grad_query, grad_key, grad_value, lax.optimization_barrier(jnp.sum(gain_parts, axis=0)))
```

```python
import jax
import jax.numpy as jnp
from jax import lax
from jax.sharding import PartitionSpec as P

HEADS = 12
HEAD_DIM = 128
BLOCK = 256


norm_eps = 1e-05


def carried_in(value, axis, backward, extra=None):
    count = lax.axis_size(axis)
    rows = value.reshape(count, -1)
    width = rows.shape[1]
    if extra is not None:
        rows = jnp.concatenate([rows, extra.reshape(count, -1)], axis=1)
    parts = lax.all_to_all(rows, axis, 0, 0)
    if backward:
        parts = parts[::-1]
    running = jnp.cumsum(parts, axis=0)
    shifted = jnp.concatenate([jnp.zeros_like(running[:1]), running[:-1]], axis=0)
    if extra is not None:
        total = jnp.broadcast_to(running[-1:, width:], (count, rows.shape[1] - width))
        shifted = jnp.concatenate([shifted[:, :width], total], axis=1)
    if backward:
        shifted = shifted[::-1]
    back = lax.all_to_all(shifted, axis, 0, 0)
    state = back[:, :width].reshape(value.shape)
    if extra is None:
        return state
    return state, back[:, width:].reshape(extra.shape)


def lower_mask(length):
    row_index = lax.broadcasted_iota(jnp.int32, (length, length), 0)
    col_index = lax.broadcasted_iota(jnp.int32, (length, length), 1)
    return row_index >= col_index


def local(query_rows, key_rows, value_rows, norm_gain, grad_output):
    tokens = query_rows.shape[1]
    features = query_rows.shape[2]
    blocks = tokens // BLOCK
    block_shape = (blocks, BLOCK, HEADS, HEAD_DIM)
    queries = query_rows.reshape(block_shape)
    key_blocks = key_rows.reshape(block_shape)
    value_blocks = value_rows.reshape(block_shape)
    causal = lower_mask(BLOCK)
    local_states = jnp.einsum(
        "nchd,nche->nhde", key_blocks, value_blocks, preferred_element_type=jnp.float32
    )
    device_total = jnp.sum(local_states, axis=0)
    carried = carried_in(device_total, "seq", False)
    running = jnp.cumsum(local_states, axis=0)
    before = jnp.concatenate([local_states[:1] * 0.0, running[:-1]], axis=0)
    states = (carried[None] + before).astype(jnp.bfloat16)
    scores = jnp.einsum("nchd,nthd->nhct", queries, key_blocks, preferred_element_type=jnp.float32)
    weights = jnp.where(causal, scores, 0.0).astype(jnp.bfloat16)
    combined = jnp.einsum("nchd,nhde->nche", queries, states, preferred_element_type=jnp.float32)
    combined = combined + jnp.einsum(
        "nhct,nthe->nche", weights, value_blocks, preferred_element_type=jnp.float32
    )
    combined = combined.reshape(1, tokens, features)
    inverse = lax.rsqrt(jnp.mean(combined * combined, axis=-1, keepdims=True) + norm_eps)
    normed = combined * inverse
    attended = (normed * norm_gain).astype(jnp.bfloat16)
    upstream = grad_output.astype(jnp.float32)
    gain_terms = jnp.sum(upstream * normed, axis=(0, 1))
    grad_normed = upstream * norm_gain
    grad_combined = inverse * (
        grad_normed - normed * jnp.mean(grad_normed * normed, axis=-1, keepdims=True)
    )
    grad_blocks = grad_combined.astype(jnp.bfloat16).reshape(block_shape)
    query_parts = jnp.einsum(
        "nchd,nche->nhde", queries, grad_blocks, preferred_element_type=jnp.float32
    )
    suffix, gain_seq = carried_in(jnp.sum(query_parts, axis=0), "seq", True, gain_terms)
    grad_gain = lax.psum(gain_seq, "dp")
    from_end = jnp.cumsum(query_parts[::-1], axis=0)[::-1]
    behind = jnp.concatenate([from_end[1:], jnp.zeros_like(query_parts)], axis=0)
    suffix_states = (suffix[None] + behind).astype(jnp.bfloat16)
    grad_scores = jnp.einsum(
        "nche,nthe->nhct", grad_blocks, value_blocks, preferred_element_type=jnp.float32
    )
    grad_weights = jnp.where(causal, grad_scores, 0.0).astype(jnp.bfloat16)
    grad_query = jnp.einsum(
        "nche,nhde->nchd", grad_blocks, states, preferred_element_type=jnp.float32
    )
    grad_query = grad_query + jnp.einsum(
        "nhct,nthd->nchd", grad_weights, key_blocks, preferred_element_type=jnp.float32
    )
    grad_key = jnp.einsum(
        "nche,nhde->nchd", value_blocks, suffix_states, preferred_element_type=jnp.float32
    )
    grad_key = grad_key + jnp.einsum(
        "nhct,nchd->nthd", grad_weights, queries, preferred_element_type=jnp.float32
    )
    grad_value = jnp.einsum(
        "nchd,nhde->nche", key_blocks, suffix_states, preferred_element_type=jnp.float32
    )
    grad_value = grad_value + jnp.einsum(
        "nhct,nche->nthe", weights, grad_blocks, preferred_element_type=jnp.float32
    )
    out_shape = (1, tokens, features)
    return (
        attended,
        grad_query.reshape(out_shape).astype(jnp.bfloat16),
        grad_key.reshape(out_shape).astype(jnp.bfloat16),
        grad_value.reshape(out_shape).astype(jnp.bfloat16),
        grad_gain,
    )


def solution(mesh):
    placed = (
        P("dp", "seq", None),
        P("dp", "seq", None),
        P("dp", "seq", None),
        P(),
        P("dp", "seq", None),
    )
    return jax.shard_map(
        local,
        mesh=mesh,
        in_specs=placed,
        out_specs=(
            P("dp", "seq", None),
            P("dp", "seq", None),
            P("dp", "seq", None),
            P("dp", "seq", None),
            P(),
        ),
        check_vma=False,
    )
```

```python
import jax
import jax.numpy as jnp
from jax import lax
from jax.sharding import PartitionSpec as P

HEADS = 12
HEAD_DIM = 128
BLOCK = 256


norm_eps = 1e-05


def carried_in(value, axis, backward, extra=None):
    count = lax.axis_size(axis)
    lanes = value.shape[-1]
    rows = value.reshape(count, -1, lanes)
    depth = rows.shape[1]
    if extra is not None:
        spread = extra.reshape(count, 1, -1)
        spread = jnp.pad(spread, ((0, 0), (0, 0), (0, lanes - spread.shape[2])))
        rows = jnp.concatenate([rows, spread], axis=1)
    parts = lax.all_to_all(rows, axis, 0, 0)
    running = lax.cumsum(parts, axis=0, reverse=backward)
    empty = jnp.zeros_like(running[:1])
    if backward:
        shifted = jnp.concatenate([running[1:], empty], axis=0)
    else:
        shifted = jnp.concatenate([empty, running[:-1]], axis=0)
    if extra is not None:
        total = running[-1:] if not backward else running[:1]
        row = lax.broadcasted_iota(jnp.int32, shifted.shape, 1)
        shifted = jnp.where(row < depth, shifted, total)
    back = lax.all_to_all(shifted, axis, 0, 0)
    state = back[:, :depth].reshape(value.shape)
    if extra is None:
        return state
    return state, back[:, depth, : extra.size // count].reshape(extra.shape)


def lower_mask(length):
    row_index = lax.broadcasted_iota(jnp.int32, (length, length), 0)
    col_index = lax.broadcasted_iota(jnp.int32, (length, length), 1)
    return row_index >= col_index


def local(query_rows, key_rows, value_rows, norm_gain, grad_output):
    tokens = query_rows.shape[1]
    features = query_rows.shape[2]
    blocks = tokens // BLOCK
    block_shape = (blocks, BLOCK, HEADS, HEAD_DIM)
    queries = query_rows.reshape(block_shape)
    key_blocks = key_rows.reshape(block_shape)
    value_blocks = value_rows.reshape(block_shape)
    causal = lower_mask(BLOCK)
    local_states = jnp.einsum(
        "nchd,nche->nhde", key_blocks, value_blocks, preferred_element_type=jnp.float32
    )
    device_total = jnp.sum(local_states, axis=0)
    carried = carried_in(device_total, "seq", False)
    running = jnp.cumsum(local_states, axis=0)
    before = jnp.concatenate([local_states[:1] * 0.0, running[:-1]], axis=0)
    states = (carried[None] + before).astype(jnp.bfloat16)
    scores = jnp.einsum("nchd,nthd->nhct", queries, key_blocks, preferred_element_type=jnp.float32)
    weights = jnp.where(causal, scores, 0.0).astype(jnp.bfloat16)
    combined = jnp.einsum("nchd,nhde->nche", queries, states, preferred_element_type=jnp.float32)
    combined = combined + jnp.einsum(
        "nhct,nthe->nche", weights, value_blocks, preferred_element_type=jnp.float32
    )
    combined = combined.reshape(1, tokens, features)
    inverse = lax.rsqrt(jnp.mean(combined * combined, axis=-1, keepdims=True) + norm_eps)
    normed = combined * inverse
    attended = (normed * norm_gain).astype(jnp.bfloat16)
    upstream = grad_output.astype(jnp.float32)
    gain_terms = jnp.sum(upstream * normed, axis=(0, 1))
    grad_normed = upstream * norm_gain
    grad_combined = inverse * (
        grad_normed - normed * jnp.mean(grad_normed * normed, axis=-1, keepdims=True)
    )
    grad_blocks = grad_combined.astype(jnp.bfloat16).reshape(block_shape)
    query_parts = jnp.einsum(
        "nchd,nche->nhde", queries, grad_blocks, preferred_element_type=jnp.float32
    )
    suffix, gain_seq = carried_in(jnp.sum(query_parts, axis=0), "seq", True, gain_terms)
    grad_gain = lax.psum(gain_seq, "dp")
    from_end = jnp.cumsum(query_parts[::-1], axis=0)[::-1]
    behind = jnp.concatenate([from_end[1:], jnp.zeros_like(query_parts)], axis=0)
    suffix_states = (suffix[None] + behind).astype(jnp.bfloat16)
    grad_scores = jnp.einsum(
        "nche,nthe->nhct", grad_blocks, value_blocks, preferred_element_type=jnp.float32
    )
    grad_weights = jnp.where(causal, grad_scores, 0.0).astype(jnp.bfloat16)
    grad_query = jnp.einsum(
        "nche,nhde->nchd", grad_blocks, states, preferred_element_type=jnp.float32
    )
    grad_query = grad_query + jnp.einsum(
        "nhct,nthd->nchd", grad_weights, key_blocks, preferred_element_type=jnp.float32
    )
    grad_key = jnp.einsum(
        "nche,nhde->nchd", value_blocks, suffix_states, preferred_element_type=jnp.float32
    )
    grad_key = grad_key + jnp.einsum(
        "nhct,nchd->nthd", grad_weights, queries, preferred_element_type=jnp.float32
    )
    grad_value = jnp.einsum(
        "nchd,nhde->nche", key_blocks, suffix_states, preferred_element_type=jnp.float32
    )
    grad_value = grad_value + jnp.einsum(
        "nhct,nche->nthe", weights, grad_blocks, preferred_element_type=jnp.float32
    )
    out_shape = (1, tokens, features)
    return (
        attended,
        grad_query.reshape(out_shape).astype(jnp.bfloat16),
        grad_key.reshape(out_shape).astype(jnp.bfloat16),
        grad_value.reshape(out_shape).astype(jnp.bfloat16),
        grad_gain,
    )


def solution(mesh):
    placed = (
        P("dp", "seq", None),
        P("dp", "seq", None),
        P("dp", "seq", None),
        P(),
        P("dp", "seq", None),
    )
    return jax.shard_map(
        local,
        mesh=mesh,
        in_specs=placed,
        out_specs=(
            P("dp", "seq", None),
            P("dp", "seq", None),
            P("dp", "seq", None),
            P("dp", "seq", None),
            P(),
        ),
        check_vma=False,
    )
```

```python
import jax
import jax.numpy as jnp
from jax import lax
from jax.sharding import PartitionSpec as P

HEADS = 12
HEAD_DIM = 128
BLOCK = 256


norm_eps = 1e-05


def carried_in(value, axis, backward):
    count = lax.axis_size(axis)
    lanes = value.shape[-1]
    rows = value.reshape(count, -1, lanes)
    parts = lax.all_to_all(rows, axis, 0, 0)
    running = lax.cumsum(parts, axis=0, reverse=backward)
    empty = jnp.zeros_like(running[:1])
    if backward:
        shifted = jnp.concatenate([running[1:], empty], axis=0)
    else:
        shifted = jnp.concatenate([empty, running[:-1]], axis=0)
    back = lax.all_to_all(shifted, axis, 0, 0)
    return back.reshape(value.shape)


def butterfly_sum(value, axis):
    count = lax.axis_size(axis)
    step = 1
    while step < count:
        value = value + lax.ppermute(value, axis, [(i, i ^ step) for i in range(count)])
        step *= 2
    return value


def lower_mask(length):
    row_index = lax.broadcasted_iota(jnp.int32, (length, length), 0)
    col_index = lax.broadcasted_iota(jnp.int32, (length, length), 1)
    return row_index >= col_index


def local(query_rows, key_rows, value_rows, norm_gain, grad_output):
    tokens = query_rows.shape[1]
    features = query_rows.shape[2]
    blocks = tokens // BLOCK
    block_shape = (blocks, BLOCK, HEADS, HEAD_DIM)
    queries = query_rows.reshape(block_shape)
    key_blocks = key_rows.reshape(block_shape)
    value_blocks = value_rows.reshape(block_shape)
    causal = lower_mask(BLOCK)
    local_states = jnp.einsum(
        "nchd,nche->nhde", key_blocks, value_blocks, preferred_element_type=jnp.float32
    )
    device_total = jnp.sum(local_states, axis=0)
    carried = carried_in(device_total, "seq", False)
    running = jnp.cumsum(local_states, axis=0)
    before = jnp.concatenate([local_states[:1] * 0.0, running[:-1]], axis=0)
    states = (carried[None] + before).astype(jnp.bfloat16)
    scores = jnp.einsum("nchd,nthd->nhct", queries, key_blocks, preferred_element_type=jnp.float32)
    weights = jnp.where(causal, scores, 0.0).astype(jnp.bfloat16)
    combined = jnp.einsum("nchd,nhde->nche", queries, states, preferred_element_type=jnp.float32)
    combined = combined + jnp.einsum(
        "nhct,nthe->nche", weights, value_blocks, preferred_element_type=jnp.float32
    )
    combined = combined.reshape(1, tokens, features)
    inverse = lax.rsqrt(jnp.mean(combined * combined, axis=-1, keepdims=True) + norm_eps)
    normed = combined * inverse
    attended = (normed * norm_gain).astype(jnp.bfloat16)
    upstream = grad_output.astype(jnp.float32)
    gain_terms = jnp.sum(upstream * normed, axis=(0, 1))
    grad_normed = upstream * norm_gain
    grad_combined = inverse * (
        grad_normed - normed * jnp.mean(grad_normed * normed, axis=-1, keepdims=True)
    )
    grad_blocks = grad_combined.astype(jnp.bfloat16).reshape(block_shape)
    query_parts = jnp.einsum(
        "nchd,nche->nhde", queries, grad_blocks, preferred_element_type=jnp.float32
    )
    suffix = carried_in(jnp.sum(query_parts, axis=0), "seq", True)
    grad_gain = butterfly_sum(butterfly_sum(gain_terms, "dp"), "seq")
    from_end = lax.cumsum(query_parts, axis=0, reverse=True)
    behind = jnp.concatenate([from_end[1:], query_parts[-1:] * 0.0], axis=0)
    suffix_states = (suffix[None] + behind).astype(jnp.bfloat16)
    grad_scores = jnp.einsum(
        "nche,nthe->nhct", grad_blocks, value_blocks, preferred_element_type=jnp.float32
    )
    grad_weights = jnp.where(causal, grad_scores, 0.0).astype(jnp.bfloat16)
    grad_query = jnp.einsum(
        "nche,nhde->nchd", grad_blocks, states, preferred_element_type=jnp.float32
    )
    grad_query = grad_query + jnp.einsum(
        "nhct,nthd->nchd", grad_weights, key_blocks, preferred_element_type=jnp.float32
    )
    grad_key = jnp.einsum(
        "nche,nhde->nchd", value_blocks, suffix_states, preferred_element_type=jnp.float32
    )
    grad_key = grad_key + jnp.einsum(
        "nhct,nchd->nthd", grad_weights, queries, preferred_element_type=jnp.float32
    )
    grad_value = jnp.einsum(
        "nchd,nhde->nche", key_blocks, suffix_states, preferred_element_type=jnp.float32
    )
    grad_value = grad_value + jnp.einsum(
        "nhct,nche->nthe", weights, grad_blocks, preferred_element_type=jnp.float32
    )
    out_shape = (1, tokens, features)
    return (
        attended,
        grad_query.reshape(out_shape).astype(jnp.bfloat16),
        grad_key.reshape(out_shape).astype(jnp.bfloat16),
        grad_value.reshape(out_shape).astype(jnp.bfloat16),
        grad_gain,
    )


def solution(mesh):
    placed = (
        P("dp", "seq", None),
        P("dp", "seq", None),
        P("dp", "seq", None),
        P(),
        P("dp", "seq", None),
    )
    return jax.shard_map(
        local,
        mesh=mesh,
        in_specs=placed,
        out_specs=(
            P("dp", "seq", None),
            P("dp", "seq", None),
            P("dp", "seq", None),
            P("dp", "seq", None),
            P(),
        ),
        check_vma=False,
    )
```

```python
import jax
import jax.numpy as jnp
from jax import lax
from jax.sharding import PartitionSpec as P

HEADS = 12
HEAD_DIM = 128
BLOCK = 256


norm_eps = 1e-05


def carried_in(value, axis, backward):
    count = lax.axis_size(axis)
    lanes = value.shape[-1]
    rows = value.reshape(count, -1, lanes)
    parts = lax.all_to_all(rows, axis, 0, 0)
    row = lax.broadcasted_iota(jnp.int32, (count, count), 0)
    col = lax.broadcasted_iota(jnp.int32, (count, count), 1)
    strict = (row < col) if backward else (row > col)
    shifted = jnp.einsum(
        "ij,jkl->ikl",
        strict.astype(jnp.float32),
        parts,
        precision=lax.Precision.HIGHEST,
        preferred_element_type=jnp.float32,
    )
    back = lax.all_to_all(shifted, axis, 0, 0)
    return back.reshape(value.shape)


def butterfly_sum(value, axis, first=1, last=None):
    count = lax.axis_size(axis)
    last = count if last is None else last
    step = first
    while step < last:
        value = value + lax.ppermute(value, axis, [(i, i ^ step) for i in range(count)])
        step *= 2
    return value


def lower_mask(length):
    row_index = lax.broadcasted_iota(jnp.int32, (length, length), 0)
    col_index = lax.broadcasted_iota(jnp.int32, (length, length), 1)
    return row_index >= col_index


def local(query_rows, key_rows, value_rows, norm_gain, grad_output):
    tokens = query_rows.shape[1]
    features = query_rows.shape[2]
    blocks = tokens // BLOCK
    block_shape = (blocks, BLOCK, HEADS, HEAD_DIM)
    queries = query_rows.reshape(block_shape)
    key_blocks = key_rows.reshape(block_shape)
    value_blocks = value_rows.reshape(block_shape)
    causal = lower_mask(BLOCK)
    local_states = jnp.einsum(
        "nchd,nche->nhde", key_blocks, value_blocks, preferred_element_type=jnp.float32
    )
    device_total = jnp.sum(local_states, axis=0)
    carried = carried_in(device_total, "seq", False)
    running = jnp.cumsum(local_states, axis=0)
    before = jnp.concatenate([local_states[:1] * 0.0, running[:-1]], axis=0)
    states = (carried[None] + before).astype(jnp.bfloat16)
    scores = jnp.einsum("nchd,nthd->nhct", queries, key_blocks, preferred_element_type=jnp.float32)
    weights = jnp.where(causal, scores, 0.0).astype(jnp.bfloat16)
    combined = jnp.einsum("nchd,nhde->nche", queries, states, preferred_element_type=jnp.float32)
    combined = combined + jnp.einsum(
        "nhct,nthe->nche", weights, value_blocks, preferred_element_type=jnp.float32
    )
    combined = combined.reshape(1, tokens, features)
    inverse = lax.rsqrt(jnp.mean(combined * combined, axis=-1, keepdims=True) + norm_eps)
    normed = combined * inverse
    attended = (normed * norm_gain).astype(jnp.bfloat16)
    upstream = grad_output.astype(jnp.float32)
    gain_terms = jnp.sum(upstream * normed, axis=(0, 1))
    grad_normed = upstream * norm_gain
    grad_combined = inverse * (
        grad_normed - normed * jnp.mean(grad_normed * normed, axis=-1, keepdims=True)
    )
    grad_blocks = grad_combined.astype(jnp.bfloat16).reshape(block_shape)
    query_parts = jnp.einsum(
        "nchd,nche->nhde", queries, grad_blocks, preferred_element_type=jnp.float32
    )
    suffix = carried_in(jnp.sum(query_parts, axis=0), "seq", True)
    gain_near = butterfly_sum(butterfly_sum(gain_terms, "dp"), "seq", 1, 4)
    grad_gain = butterfly_sum(gain_near, "seq", 4)
    from_end = lax.cumsum(query_parts, axis=0, reverse=True)
    behind = jnp.concatenate([from_end[1:], query_parts[-1:] * 0.0], axis=0)
    suffix_states = (suffix[None] + behind).astype(jnp.bfloat16)
    grad_scores = jnp.einsum(
        "nche,nthe->nhct", grad_blocks, value_blocks, preferred_element_type=jnp.float32
    )
    grad_weights = jnp.where(causal, grad_scores, 0.0).astype(jnp.bfloat16)
    grad_query = jnp.einsum(
        "nche,nhde->nchd", grad_blocks, states, preferred_element_type=jnp.float32
    )
    grad_query = grad_query + jnp.einsum(
        "nhct,nthd->nchd", grad_weights, key_blocks, preferred_element_type=jnp.float32
    )
    grad_key = jnp.einsum(
        "nche,nhde->nchd", value_blocks, suffix_states, preferred_element_type=jnp.float32
    )
    grad_key = grad_key + jnp.einsum(
        "nhct,nchd->nthd", grad_weights, queries, preferred_element_type=jnp.float32
    )
    grad_value = jnp.einsum(
        "nchd,nhde->nche", key_blocks, suffix_states, preferred_element_type=jnp.float32
    )
    grad_value = grad_value + jnp.einsum(
        "nhct,nche->nthe", weights, grad_blocks, preferred_element_type=jnp.float32
    )
    out_shape = (1, tokens, features)
    return (
        attended,
        grad_query.reshape(out_shape).astype(jnp.bfloat16),
        grad_key.reshape(out_shape).astype(jnp.bfloat16),
        grad_value.reshape(out_shape).astype(jnp.bfloat16),
        grad_gain,
    )


def solution(mesh):
    placed = (
        P("dp", "seq", None),
        P("dp", "seq", None),
        P("dp", "seq", None),
        P(),
        P("dp", "seq", None),
    )
    return jax.shard_map(
        local,
        mesh=mesh,
        in_specs=placed,
        out_specs=(
            P("dp", "seq", None),
            P("dp", "seq", None),
            P("dp", "seq", None),
            P("dp", "seq", None),
            P(),
        ),
        check_vma=False,
    )
```

```python
import jax
import jax.numpy as jnp
from jax import lax
from jax.sharding import PartitionSpec as P

HEADS = 12
HEAD_DIM = 128
BLOCK = 256


norm_eps = 1e-05


def carried_in(value, axis, backward, after=None):
    count = lax.axis_size(axis)
    rows = value.reshape(count, -1)
    parts = lax.all_to_all(rows, axis, 0, 0)
    row = lax.broadcasted_iota(jnp.int32, (count, count), 0)
    col = lax.broadcasted_iota(jnp.int32, (count, count), 1)
    strict = ((row < col) if backward else (row > col)).astype(jnp.float32)
    if after is not None:
        strict = strict + 0.0 * after
    shifted = jnp.einsum(
        "ij,jk->ik",
        strict,
        parts,
        precision=lax.Precision.HIGHEST,
        preferred_element_type=jnp.float32,
    )
    back = lax.all_to_all(shifted, axis, 0, 0)
    return back.reshape(value.shape)


def butterfly_sum(value, axis, first=1, last=None):
    count = lax.axis_size(axis)
    last = count if last is None else last
    step = first
    while step < last:
        value = value + lax.ppermute(value, axis, [(i, i ^ step) for i in range(count)])
        step *= 2
    return value


def lower_mask(length):
    row_index = lax.broadcasted_iota(jnp.int32, (length, length), 0)
    col_index = lax.broadcasted_iota(jnp.int32, (length, length), 1)
    return row_index >= col_index


def local(query_rows, key_rows, value_rows, norm_gain, grad_output):
    tokens = query_rows.shape[1]
    features = query_rows.shape[2]
    blocks = tokens // BLOCK
    block_shape = (blocks, BLOCK, HEADS, HEAD_DIM)
    queries = query_rows.reshape(block_shape)
    key_blocks = key_rows.reshape(block_shape)
    value_blocks = value_rows.reshape(block_shape)
    causal = lower_mask(BLOCK)
    local_states = jnp.einsum(
        "nchd,nche->nhde", key_blocks, value_blocks, preferred_element_type=jnp.float32
    )
    device_total = jnp.sum(local_states, axis=0)
    carried = carried_in(device_total, "seq", False)
    running = jnp.cumsum(local_states, axis=0)
    before = jnp.concatenate([local_states[:1] * 0.0, running[:-1]], axis=0)
    states = (carried[None] + before).astype(jnp.bfloat16)
    scores = jnp.einsum("nchd,nthd->nhct", queries, key_blocks, preferred_element_type=jnp.float32)
    weights = jnp.where(causal, scores, 0.0).astype(jnp.bfloat16)
    combined = jnp.einsum("nchd,nhde->nche", queries, states, preferred_element_type=jnp.float32)
    combined = combined + jnp.einsum(
        "nhct,nthe->nche", weights, value_blocks, preferred_element_type=jnp.float32
    )
    combined = combined.reshape(1, tokens, features)
    inverse = lax.rsqrt(jnp.mean(combined * combined, axis=-1, keepdims=True) + norm_eps)
    normed = combined * inverse
    attended = (normed * norm_gain).astype(jnp.bfloat16)
    upstream = grad_output.astype(jnp.float32)
    gain_terms = jnp.sum(upstream * normed, axis=(0, 1))
    grad_normed = upstream * norm_gain
    grad_combined = inverse * (
        grad_normed - normed * jnp.mean(grad_normed * normed, axis=-1, keepdims=True)
    )
    grad_blocks = grad_combined.astype(jnp.bfloat16).reshape(block_shape)
    query_parts = jnp.einsum(
        "nchd,nche->nhde", queries, grad_blocks, preferred_element_type=jnp.float32
    )
    gain_near = butterfly_sum(butterfly_sum(gain_terms, "dp"), "seq", 1, 4)
    suffix = carried_in(jnp.sum(query_parts, axis=0), "seq", True, gain_near[0])
    grad_gain = butterfly_sum(gain_near, "seq", 4)
    from_end = lax.cumsum(query_parts, axis=0, reverse=True)
    behind = jnp.concatenate([from_end[1:], query_parts[-1:] * 0.0], axis=0)
    suffix_states = (suffix[None] + behind).astype(jnp.bfloat16)
    grad_scores = jnp.einsum(
        "nche,nthe->nhct", grad_blocks, value_blocks, preferred_element_type=jnp.float32
    )
    grad_weights = jnp.where(causal, grad_scores, 0.0).astype(jnp.bfloat16)
    grad_query = jnp.einsum(
        "nche,nhde->nchd", grad_blocks, states, preferred_element_type=jnp.float32
    )
    grad_query = grad_query + jnp.einsum(
        "nhct,nthd->nchd", grad_weights, key_blocks, preferred_element_type=jnp.float32
    )
    grad_key = jnp.einsum(
        "nche,nhde->nchd", value_blocks, suffix_states, preferred_element_type=jnp.float32
    )
    grad_key = grad_key + jnp.einsum(
        "nhct,nchd->nthd", grad_weights, queries, preferred_element_type=jnp.float32
    )
    grad_value = jnp.einsum(
        "nchd,nhde->nche", key_blocks, suffix_states, preferred_element_type=jnp.float32
    )
    grad_value = grad_value + jnp.einsum(
        "nhct,nche->nthe", weights, grad_blocks, preferred_element_type=jnp.float32
    )
    out_shape = (1, tokens, features)
    return (
        attended,
        grad_query.reshape(out_shape).astype(jnp.bfloat16),
        grad_key.reshape(out_shape).astype(jnp.bfloat16),
        grad_value.reshape(out_shape).astype(jnp.bfloat16),
        grad_gain,
    )


def solution(mesh):
    placed = (
        P("dp", "seq", None),
        P("dp", "seq", None),
        P("dp", "seq", None),
        P(),
        P("dp", "seq", None),
    )
    return jax.shard_map(
        local,
        mesh=mesh,
        in_specs=placed,
        out_specs=(
            P("dp", "seq", None),
            P("dp", "seq", None),
            P("dp", "seq", None),
            P("dp", "seq", None),
            P(),
        ),
        check_vma=False,
    )
```

```python
import jax
import jax.numpy as jnp
from jax import lax
from jax.sharding import PartitionSpec as P

HEADS = 12
HEAD_DIM = 128
BLOCK = 256


norm_eps = 1e-05


def carried_in(value, axis, backward):
    count = lax.axis_size(axis)
    lanes = value.shape[-1]
    rows = value.reshape(count, -1, lanes)
    parts = lax.all_to_all(rows, axis, 0, 0)
    row = lax.broadcasted_iota(jnp.int32, (count, count), 0)
    col = lax.broadcasted_iota(jnp.int32, (count, count), 1)
    strict = (row < col) if backward else (row > col)
    shifted = jnp.einsum(
        "ij,jkl->ikl",
        strict.astype(jnp.float32),
        parts,
        precision=lax.Precision.HIGHEST,
        preferred_element_type=jnp.float32,
    )
    back = lax.all_to_all(shifted, axis, 0, 0)
    return back.reshape(value.shape)


def butterfly_sum(value, axis, first=1, last=None):
    count = lax.axis_size(axis)
    last = count if last is None else last
    step = first
    while step < last:
        value = value + lax.ppermute(value, axis, [(i, i ^ step) for i in range(count)])
        step *= 2
    return value


def lower_mask(length):
    row_index = lax.broadcasted_iota(jnp.int32, (length, length), 0)
    col_index = lax.broadcasted_iota(jnp.int32, (length, length), 1)
    return row_index >= col_index


def local(query_rows, key_rows, value_rows, norm_gain, grad_output):
    tokens = query_rows.shape[1]
    features = query_rows.shape[2]
    blocks = tokens // BLOCK
    block_shape = (blocks, BLOCK, HEADS, HEAD_DIM)
    queries = query_rows.reshape(block_shape)
    key_blocks = key_rows.reshape(block_shape)
    value_blocks = value_rows.reshape(block_shape)
    causal = lower_mask(BLOCK)
    local_states = jnp.einsum(
        "nchd,nche->nhde", key_blocks, value_blocks, preferred_element_type=jnp.float32
    )
    device_total = jnp.sum(local_states, axis=0)
    carried = carried_in(device_total, "seq", False)
    running = jnp.cumsum(local_states, axis=0)
    before = jnp.concatenate([local_states[:1] * 0.0, running[:-1]], axis=0)
    states = (carried[None] + before).astype(jnp.bfloat16)
    scores = jnp.einsum("nchd,nthd->nhct", queries, key_blocks, preferred_element_type=jnp.float32)
    weights = jnp.where(causal, scores, 0.0).astype(jnp.bfloat16)
    combined = jnp.einsum("nchd,nhde->nche", queries, states, preferred_element_type=jnp.float32)
    combined = combined + jnp.einsum(
        "nhct,nthe->nche", weights, value_blocks, preferred_element_type=jnp.float32
    )
    combined = combined.reshape(1, tokens, features)
    inverse = lax.rsqrt(jnp.mean(combined * combined, axis=-1, keepdims=True) + norm_eps)
    normed = combined * inverse
    attended = (normed * norm_gain).astype(jnp.bfloat16)
    upstream = grad_output.astype(jnp.float32)
    gain_terms = jnp.sum(upstream * normed, axis=(0, 1))
    grad_normed = upstream * norm_gain
    grad_combined = inverse * (
        grad_normed - normed * jnp.mean(grad_normed * normed, axis=-1, keepdims=True)
    )
    grad_blocks = grad_combined.astype(jnp.bfloat16).reshape(block_shape)
    query_parts = jnp.einsum(
        "nchd,nche->nhde", queries, grad_blocks, preferred_element_type=jnp.float32
    )
    suffix = carried_in(jnp.sum(query_parts, axis=0), "seq", True)
    gain_dp = butterfly_sum(gain_terms, "dp")
    grad_gain = jnp.sum(lax.all_gather(gain_dp, "seq"), axis=0)
    from_end = lax.cumsum(query_parts, axis=0, reverse=True)
    behind = jnp.concatenate([from_end[1:], query_parts[-1:] * 0.0], axis=0)
    suffix_states = (suffix[None] + behind).astype(jnp.bfloat16)
    grad_scores = jnp.einsum(
        "nche,nthe->nhct", grad_blocks, value_blocks, preferred_element_type=jnp.float32
    )
    grad_weights = jnp.where(causal, grad_scores, 0.0).astype(jnp.bfloat16)
    grad_query = jnp.einsum(
        "nche,nhde->nchd", grad_blocks, states, preferred_element_type=jnp.float32
    )
    grad_query = grad_query + jnp.einsum(
        "nhct,nthd->nchd", grad_weights, key_blocks, preferred_element_type=jnp.float32
    )
    grad_key = jnp.einsum(
        "nche,nhde->nchd", value_blocks, suffix_states, preferred_element_type=jnp.float32
    )
    grad_key = grad_key + jnp.einsum(
        "nhct,nchd->nthd", grad_weights, queries, preferred_element_type=jnp.float32
    )
    grad_value = jnp.einsum(
        "nchd,nhde->nche", key_blocks, suffix_states, preferred_element_type=jnp.float32
    )
    grad_value = grad_value + jnp.einsum(
        "nhct,nche->nthe", weights, grad_blocks, preferred_element_type=jnp.float32
    )
    out_shape = (1, tokens, features)
    return (
        attended,
        grad_query.reshape(out_shape).astype(jnp.bfloat16),
        grad_key.reshape(out_shape).astype(jnp.bfloat16),
        grad_value.reshape(out_shape).astype(jnp.bfloat16),
        grad_gain,
    )


def solution(mesh):
    placed = (
        P("dp", "seq", None),
        P("dp", "seq", None),
        P("dp", "seq", None),
        P(),
        P("dp", "seq", None),
    )
    return jax.shard_map(
        local,
        mesh=mesh,
        in_specs=placed,
        out_specs=(
            P("dp", "seq", None),
            P("dp", "seq", None),
            P("dp", "seq", None),
            P("dp", "seq", None),
            P(),
        ),
        check_vma=False,
    )
```

```python
import jax
import jax.numpy as jnp
from jax import lax
from jax.sharding import PartitionSpec as P

HEADS = 12
HEAD_DIM = 128
BLOCK = 256
GAIN_PAD = 16384


norm_eps = 1e-05


def carried_in(value, axis, backward):
    count = lax.axis_size(axis)
    lanes = value.shape[-1]
    rows = value.reshape(count, -1, lanes)
    parts = lax.all_to_all(rows, axis, 0, 0)
    row = lax.broadcasted_iota(jnp.int32, (count, count), 0)
    col = lax.broadcasted_iota(jnp.int32, (count, count), 1)
    strict = (row < col) if backward else (row > col)
    shifted = jnp.einsum(
        "ij,jkl->ikl",
        strict.astype(jnp.float32),
        parts,
        precision=lax.Precision.HIGHEST,
        preferred_element_type=jnp.float32,
    )
    back = lax.all_to_all(shifted, axis, 0, 0)
    return back.reshape(value.shape)


def lower_mask(length):
    row_index = lax.broadcasted_iota(jnp.int32, (length, length), 0)
    col_index = lax.broadcasted_iota(jnp.int32, (length, length), 1)
    return row_index >= col_index


def local(query_rows, key_rows, value_rows, norm_gain, grad_output):
    tokens = query_rows.shape[1]
    features = query_rows.shape[2]
    blocks = tokens // BLOCK
    block_shape = (blocks, BLOCK, HEADS, HEAD_DIM)
    queries = query_rows.reshape(block_shape)
    key_blocks = key_rows.reshape(block_shape)
    value_blocks = value_rows.reshape(block_shape)
    causal = lower_mask(BLOCK)
    local_states = jnp.einsum(
        "nchd,nche->nhde", key_blocks, value_blocks, preferred_element_type=jnp.float32
    )
    device_total = jnp.sum(local_states, axis=0)
    carried = carried_in(device_total, "seq", False)
    running = jnp.cumsum(local_states, axis=0)
    before = jnp.concatenate([local_states[:1] * 0.0, running[:-1]], axis=0)
    states = (carried[None] + before).astype(jnp.bfloat16)
    scores = jnp.einsum("nchd,nthd->nhct", queries, key_blocks, preferred_element_type=jnp.float32)
    weights = jnp.where(causal, scores, 0.0).astype(jnp.bfloat16)
    combined = jnp.einsum("nchd,nhde->nche", queries, states, preferred_element_type=jnp.float32)
    combined = combined + jnp.einsum(
        "nhct,nthe->nche", weights, value_blocks, preferred_element_type=jnp.float32
    )
    combined = combined.reshape(1, tokens, features)
    inverse = lax.rsqrt(jnp.mean(combined * combined, axis=-1, keepdims=True) + norm_eps)
    normed = combined * inverse
    attended = (normed * norm_gain).astype(jnp.bfloat16)
    upstream = grad_output.astype(jnp.float32)
    gain_terms = jnp.sum(upstream * normed, axis=(0, 1))
    grad_normed = upstream * norm_gain
    grad_combined = inverse * (
        grad_normed - normed * jnp.mean(grad_normed * normed, axis=-1, keepdims=True)
    )
    grad_blocks = grad_combined.astype(jnp.bfloat16).reshape(block_shape)
    query_parts = jnp.einsum(
        "nchd,nche->nhde", queries, grad_blocks, preferred_element_type=jnp.float32
    )
    suffix = carried_in(jnp.sum(query_parts, axis=0), "seq", True)

    grad_gain = lax.psum(jnp.pad(gain_terms, (0, GAIN_PAD - features)), ("dp", "seq"))[:features]
    from_end = lax.cumsum(query_parts, axis=0, reverse=True)
    behind = jnp.concatenate([from_end[1:], query_parts[-1:] * 0.0], axis=0)
    suffix_states = (suffix[None] + behind).astype(jnp.bfloat16)
    grad_scores = jnp.einsum(
        "nche,nthe->nhct", grad_blocks, value_blocks, preferred_element_type=jnp.float32
    )
    grad_weights = jnp.where(causal, grad_scores, 0.0).astype(jnp.bfloat16)
    grad_query = jnp.einsum(
        "nche,nhde->nchd", grad_blocks, states, preferred_element_type=jnp.float32
    )
    grad_query = grad_query + jnp.einsum(
        "nhct,nthd->nchd", grad_weights, key_blocks, preferred_element_type=jnp.float32
    )
    grad_key = jnp.einsum(
        "nche,nhde->nchd", value_blocks, suffix_states, preferred_element_type=jnp.float32
    )
    grad_key = grad_key + jnp.einsum(
        "nhct,nchd->nthd", grad_weights, queries, preferred_element_type=jnp.float32
    )
    grad_value = jnp.einsum(
        "nchd,nhde->nche", key_blocks, suffix_states, preferred_element_type=jnp.float32
    )
    grad_value = grad_value + jnp.einsum(
        "nhct,nche->nthe", weights, grad_blocks, preferred_element_type=jnp.float32
    )
    out_shape = (1, tokens, features)
    return (
        attended,
        grad_query.reshape(out_shape).astype(jnp.bfloat16),
        grad_key.reshape(out_shape).astype(jnp.bfloat16),
        grad_value.reshape(out_shape).astype(jnp.bfloat16),
        grad_gain,
    )


def solution(mesh):
    placed = (
        P("dp", "seq", None),
        P("dp", "seq", None),
        P("dp", "seq", None),
        P(),
        P("dp", "seq", None),
    )
    return jax.shard_map(
        local,
        mesh=mesh,
        in_specs=placed,
        out_specs=(
            P("dp", "seq", None),
            P("dp", "seq", None),
            P("dp", "seq", None),
            P("dp", "seq", None),
            P(),
        ),
        check_vma=False,
    )
```

```python
import jax
import jax.numpy as jnp
from jax import lax
from jax.sharding import PartitionSpec as P

HEADS = 12
HEAD_DIM = 128
BLOCK = 256


norm_eps = 1e-05


def carried_in(value, axis, backward, after=None):
    count = lax.axis_size(axis)
    lanes = value.shape[-1]
    rows = value.reshape(count, -1, lanes)
    parts = lax.all_to_all(rows, axis, 0, 0)
    row = lax.broadcasted_iota(jnp.int32, (count, count), 0)
    col = lax.broadcasted_iota(jnp.int32, (count, count), 1)
    strict = ((row < col) if backward else (row > col)).astype(jnp.float32)
    if after is not None:
        strict = strict + 0.0 * after
    shifted = jnp.einsum(
        "ij,jkl->ikl",
        strict,
        parts,
        precision=lax.Precision.HIGHEST,
        preferred_element_type=jnp.float32,
    )
    back = lax.all_to_all(shifted, axis, 0, 0)
    return back.reshape(value.shape)


def butterfly_sum(value, axis, first=1, last=None):
    count = lax.axis_size(axis)
    last = count if last is None else last
    step = first
    while step < last:
        value = value + lax.ppermute(value, axis, [(i, i ^ step) for i in range(count)])
        step *= 2
    return value


def lower_mask(length):
    row_index = lax.broadcasted_iota(jnp.int32, (length, length), 0)
    col_index = lax.broadcasted_iota(jnp.int32, (length, length), 1)
    return row_index >= col_index


def local_body(query_rows, key_rows, value_rows, norm_gain, grad_output):
    tokens = query_rows.shape[1]
    features = query_rows.shape[2]
    blocks = tokens // BLOCK
    block_shape = (blocks, BLOCK, HEADS, HEAD_DIM)
    queries = query_rows.reshape(block_shape)
    key_blocks = key_rows.reshape(block_shape)
    value_blocks = value_rows.reshape(block_shape)
    causal = lower_mask(BLOCK)
    local_states = jnp.einsum(
        "nchd,nche->nhde", key_blocks, value_blocks, preferred_element_type=jnp.float32
    )
    device_total = jnp.sum(local_states, axis=0)
    carried = carried_in(device_total, "seq", False)
    running = jnp.cumsum(local_states, axis=0)
    before = jnp.concatenate([local_states[:1] * 0.0, running[:-1]], axis=0)
    states = (carried[None] + before).astype(jnp.bfloat16)
    scores = jnp.einsum("nchd,nthd->nhct", queries, key_blocks, preferred_element_type=jnp.float32)
    weights = jnp.where(causal, scores, 0.0).astype(jnp.bfloat16)
    combined = jnp.einsum("nchd,nhde->nche", queries, states, preferred_element_type=jnp.float32)
    combined = combined + jnp.einsum(
        "nhct,nthe->nche", weights, value_blocks, preferred_element_type=jnp.float32
    )
    combined = combined.reshape(1, tokens, features)
    inverse = lax.rsqrt(jnp.mean(combined * combined, axis=-1, keepdims=True) + norm_eps)
    normed = combined * inverse
    attended = (normed * norm_gain).astype(jnp.bfloat16)
    upstream = grad_output.astype(jnp.float32)
    gain_terms = jnp.sum(upstream * normed, axis=(0, 1))
    grad_normed = upstream * norm_gain
    grad_combined = inverse * (
        grad_normed - normed * jnp.mean(grad_normed * normed, axis=-1, keepdims=True)
    )
    grad_blocks = grad_combined.astype(jnp.bfloat16).reshape(block_shape)
    query_parts = jnp.einsum(
        "nchd,nche->nhde", queries, grad_blocks, preferred_element_type=jnp.float32
    )
    gain_dp = butterfly_sum(gain_terms, "dp")
    suffix = carried_in(jnp.sum(query_parts, axis=0), "seq", True, gain_dp[0])
    grad_gain = butterfly_sum(gain_dp, "seq")
    from_end = lax.cumsum(query_parts, axis=0, reverse=True)
    behind = jnp.concatenate([from_end[1:], query_parts[-1:] * 0.0], axis=0)
    suffix_states = (suffix[None] + behind).astype(jnp.bfloat16)
    grad_scores = jnp.einsum(
        "nche,nthe->nhct", grad_blocks, value_blocks, preferred_element_type=jnp.float32
    )
    grad_weights = jnp.where(causal, grad_scores, 0.0).astype(jnp.bfloat16)
    grad_query = jnp.einsum(
        "nche,nhde->nchd", grad_blocks, states, preferred_element_type=jnp.float32
    )
    grad_query = grad_query + jnp.einsum(
        "nhct,nthd->nchd", grad_weights, key_blocks, preferred_element_type=jnp.float32
    )
    grad_key = jnp.einsum(
        "nche,nhde->nchd", value_blocks, suffix_states, preferred_element_type=jnp.float32
    )
    grad_key = grad_key + jnp.einsum(
        "nhct,nchd->nthd", grad_weights, queries, preferred_element_type=jnp.float32
    )
    grad_value = jnp.einsum(
        "nchd,nhde->nche", key_blocks, suffix_states, preferred_element_type=jnp.float32
    )
    grad_value = grad_value + jnp.einsum(
        "nhct,nche->nthe", weights, grad_blocks, preferred_element_type=jnp.float32
    )
    out_shape = (1, tokens, features)
    return (
        attended,
        grad_query.reshape(out_shape).astype(jnp.bfloat16),
        grad_key.reshape(out_shape).astype(jnp.bfloat16),
        grad_value.reshape(out_shape).astype(jnp.bfloat16),
        grad_gain,
    )


def solution(mesh):
    placed = (
        P("dp", "seq", None),
        P("dp", "seq", None),
        P("dp", "seq", None),
        P(),
        P("dp", "seq", None),
    )
    return jax.shard_map(
        local_body,
        mesh=mesh,
        in_specs=placed,
        out_specs=(
            P("dp", "seq", None),
            P("dp", "seq", None),
            P("dp", "seq", None),
            P("dp", "seq", None),
            P(),
        ),
        check_vma=False,
    )
```

```python
import jax
import jax.numpy as jnp
from jax import lax
from jax.sharding import PartitionSpec as P

HEADS = 12
HEAD_DIM = 128
BLOCK = 256


norm_eps = 1e-05


def carried_in(value, axis, backward, after=None):
    count = lax.axis_size(axis)
    lanes = value.shape[-1]
    rows = value.reshape(count, -1, lanes)
    parts = lax.all_to_all(rows, axis, 0, 0)
    row = lax.broadcasted_iota(jnp.int32, (count, count), 0)
    col = lax.broadcasted_iota(jnp.int32, (count, count), 1)
    strict = ((row < col) if backward else (row > col)).astype(jnp.float32)
    if after is not None:
        strict = strict + 0.0 * after
    shifted = jnp.einsum(
        "ij,jkl->ikl",
        strict,
        parts,
        precision=lax.Precision.HIGHEST,
        preferred_element_type=jnp.float32,
    )
    back = lax.all_to_all(shifted, axis, 0, 0)
    return back.reshape(value.shape)


def butterfly_sum(value, axis, radices):
    count = lax.axis_size(axis)
    step = 1
    for radix in radices:
        vals = [value] + [
            lax.ppermute(value, axis, [(i, i ^ (k * step)) for i in range(count)])
            for k in range(1, radix)
        ]
        while len(vals) > 1:
            vals = [vals[m] + vals[m + 1] for m in range(0, len(vals), 2)]
        value = vals[0]
        step *= radix
    assert step == count
    return value


def lower_mask(length):
    row_index = lax.broadcasted_iota(jnp.int32, (length, length), 0)
    col_index = lax.broadcasted_iota(jnp.int32, (length, length), 1)
    return row_index >= col_index


def local_body(query_rows, key_rows, value_rows, norm_gain, grad_output):
    tokens = query_rows.shape[1]
    features = query_rows.shape[2]
    blocks = tokens // BLOCK
    block_shape = (blocks, BLOCK, HEADS, HEAD_DIM)
    queries = query_rows.reshape(block_shape)
    key_blocks = key_rows.reshape(block_shape)
    value_blocks = value_rows.reshape(block_shape)
    causal = lower_mask(BLOCK)
    local_states = jnp.einsum(
        "nchd,nche->nhde", key_blocks, value_blocks, preferred_element_type=jnp.float32
    )
    device_total = jnp.sum(local_states, axis=0)
    carried = carried_in(device_total, "seq", False)
    running = jnp.cumsum(local_states, axis=0)
    before = jnp.concatenate([local_states[:1] * 0.0, running[:-1]], axis=0)
    states = (carried[None] + before).astype(jnp.bfloat16)
    scores = jnp.einsum("nchd,nthd->nhct", queries, key_blocks, preferred_element_type=jnp.float32)
    weights = jnp.where(causal, scores, 0.0).astype(jnp.bfloat16)
    combined = jnp.einsum("nchd,nhde->nche", queries, states, preferred_element_type=jnp.float32)
    combined = combined + jnp.einsum(
        "nhct,nthe->nche", weights, value_blocks, preferred_element_type=jnp.float32
    )
    combined = combined.reshape(1, tokens, features)
    inverse = lax.rsqrt(jnp.mean(combined * combined, axis=-1, keepdims=True) + norm_eps)
    normed = combined * inverse
    attended = (normed * norm_gain).astype(jnp.bfloat16)
    upstream = grad_output.astype(jnp.float32)
    gain_terms = jnp.sum(upstream * normed, axis=(0, 1))
    grad_normed = upstream * norm_gain
    grad_combined = inverse * (
        grad_normed - normed * jnp.mean(grad_normed * normed, axis=-1, keepdims=True)
    )
    grad_blocks = grad_combined.astype(jnp.bfloat16).reshape(block_shape)
    query_parts = jnp.einsum(
        "nchd,nche->nhde", queries, grad_blocks, preferred_element_type=jnp.float32
    )
    gain_dp = butterfly_sum(gain_terms, "dp", (8,))
    suffix = carried_in(jnp.sum(query_parts, axis=0), "seq", True, gain_dp[0])
    grad_gain = butterfly_sum(gain_dp, "seq", (4, 8))
    from_end = lax.cumsum(query_parts, axis=0, reverse=True)
    behind = jnp.concatenate([from_end[1:], query_parts[-1:] * 0.0], axis=0)
    suffix_states = (suffix[None] + behind).astype(jnp.bfloat16)
    grad_scores = jnp.einsum(
        "nche,nthe->nhct", grad_blocks, value_blocks, preferred_element_type=jnp.float32
    )
    grad_weights = jnp.where(causal, grad_scores, 0.0).astype(jnp.bfloat16)
    grad_query = jnp.einsum(
        "nche,nhde->nchd", grad_blocks, states, preferred_element_type=jnp.float32
    )
    grad_query = grad_query + jnp.einsum(
        "nhct,nthd->nchd", grad_weights, key_blocks, preferred_element_type=jnp.float32
    )
    grad_key = jnp.einsum(
        "nche,nhde->nchd", value_blocks, suffix_states, preferred_element_type=jnp.float32
    )
    grad_key = grad_key + jnp.einsum(
        "nhct,nchd->nthd", grad_weights, queries, preferred_element_type=jnp.float32
    )
    grad_value = jnp.einsum(
        "nchd,nhde->nche", key_blocks, suffix_states, preferred_element_type=jnp.float32
    )
    grad_value = grad_value + jnp.einsum(
        "nhct,nche->nthe", weights, grad_blocks, preferred_element_type=jnp.float32
    )
    out_shape = (1, tokens, features)
    return (
        attended,
        grad_query.reshape(out_shape).astype(jnp.bfloat16),
        grad_key.reshape(out_shape).astype(jnp.bfloat16),
        grad_value.reshape(out_shape).astype(jnp.bfloat16),
        grad_gain,
    )


def solution(mesh):
    placed = (
        P("dp", "seq", None),
        P("dp", "seq", None),
        P("dp", "seq", None),
        P(),
        P("dp", "seq", None),
    )
    return jax.shard_map(
        local_body,
        mesh=mesh,
        in_specs=placed,
        out_specs=(
            P("dp", "seq", None),
            P("dp", "seq", None),
            P("dp", "seq", None),
            P("dp", "seq", None),
            P(),
        ),
        check_vma=False,
    )
```

```python
import jax
import jax.numpy as jnp
from jax import lax
from jax.sharding import PartitionSpec as P

HEADS = 12
HEAD_DIM = 128
BLOCK = 256


norm_eps = 1e-05


def carried_in(value, axis, backward, after=None):
    count = lax.axis_size(axis)
    lanes = value.shape[-1]
    rows = value.reshape(count, -1, lanes)
    parts = lax.all_to_all(rows, axis, 0, 0)
    row = lax.broadcasted_iota(jnp.int32, (count, count), 0)
    col = lax.broadcasted_iota(jnp.int32, (count, count), 1)
    strict = ((row < col) if backward else (row > col)).astype(jnp.float32)
    if after is not None:
        strict = strict + 0.0 * after
    shifted = jnp.einsum(
        "ij,jkl->ikl",
        strict,
        parts,
        precision=lax.Precision.HIGHEST,
        preferred_element_type=jnp.float32,
    )
    back = lax.all_to_all(shifted, axis, 0, 0)
    return back.reshape(value.shape)


def butterfly_sum(value, axis, step=1, stop=None):
    count = lax.axis_size(axis)
    stop = count if stop is None else stop
    while step < stop:
        radix = 4 if step * 4 <= count else 2
        got = [
            lax.ppermute(value, axis, [(i, i ^ (k * step)) for i in range(count)])
            for k in range(1, radix)
        ]
        if radix == 4:
            value = (value + got[0]) + (got[1] + got[2])
        else:
            value = value + got[0]
        step *= radix
    return value


def lower_mask(length):
    row_index = lax.broadcasted_iota(jnp.int32, (length, length), 0)
    col_index = lax.broadcasted_iota(jnp.int32, (length, length), 1)
    return row_index >= col_index


def local_body(query_rows, key_rows, value_rows, norm_gain, grad_output):
    tokens = query_rows.shape[1]
    features = query_rows.shape[2]
    blocks = tokens // BLOCK
    block_shape = (blocks, BLOCK, HEADS, HEAD_DIM)
    queries = query_rows.reshape(block_shape)
    key_blocks = key_rows.reshape(block_shape)
    value_blocks = value_rows.reshape(block_shape)
    causal = lower_mask(BLOCK)
    local_states = jnp.einsum(
        "nchd,nche->nhde", key_blocks, value_blocks, preferred_element_type=jnp.float32
    )
    device_total = jnp.sum(local_states, axis=0)
    carried = carried_in(device_total, "seq", False)
    running = jnp.cumsum(local_states, axis=0)
    before = jnp.concatenate([local_states[:1] * 0.0, running[:-1]], axis=0)
    states = (carried[None] + before).astype(jnp.bfloat16)
    scores = jnp.einsum("nchd,nthd->nhct", queries, key_blocks, preferred_element_type=jnp.float32)
    weights = jnp.where(causal, scores, 0.0).astype(jnp.bfloat16)
    combined = jnp.einsum("nchd,nhde->nche", queries, states, preferred_element_type=jnp.float32)
    combined = combined + jnp.einsum(
        "nhct,nthe->nche", weights, value_blocks, preferred_element_type=jnp.float32
    )
    combined = combined.reshape(1, tokens, features)
    inverse = lax.rsqrt(jnp.mean(combined * combined, axis=-1, keepdims=True) + norm_eps)
    normed = combined * inverse
    attended = (normed * norm_gain).astype(jnp.bfloat16)
    upstream = grad_output.astype(jnp.float32)
    gain_terms = jnp.sum(upstream * normed, axis=(0, 1))
    grad_normed = upstream * norm_gain
    grad_combined = inverse * (
        grad_normed - normed * jnp.mean(grad_normed * normed, axis=-1, keepdims=True)
    )
    grad_blocks = grad_combined.astype(jnp.bfloat16).reshape(block_shape)
    query_parts = jnp.einsum(
        "nchd,nche->nhde", queries, grad_blocks, preferred_element_type=jnp.float32
    )
    gain_near = butterfly_sum(butterfly_sum(gain_terms, "dp"), "seq", 1, 4)
    suffix = carried_in(jnp.sum(query_parts, axis=0), "seq", True, gain_near[0])
    grad_gain = butterfly_sum(gain_near, "seq", 4)
    from_end = lax.cumsum(query_parts, axis=0, reverse=True)
    behind = jnp.concatenate([from_end[1:], query_parts[-1:] * 0.0], axis=0)
    suffix_states = (suffix[None] + behind).astype(jnp.bfloat16)
    grad_scores = jnp.einsum(
        "nche,nthe->nhct", grad_blocks, value_blocks, preferred_element_type=jnp.float32
    )
    grad_weights = jnp.where(causal, grad_scores, 0.0).astype(jnp.bfloat16)
    grad_query = jnp.einsum(
        "nche,nhde->nchd", grad_blocks, states, preferred_element_type=jnp.float32
    )
    grad_query = grad_query + jnp.einsum(
        "nhct,nthd->nchd", grad_weights, key_blocks, preferred_element_type=jnp.float32
    )
    grad_key = jnp.einsum(
        "nche,nhde->nchd", value_blocks, suffix_states, preferred_element_type=jnp.float32
    )
    grad_key = grad_key + jnp.einsum(
        "nhct,nchd->nthd", grad_weights, queries, preferred_element_type=jnp.float32
    )
    grad_value = jnp.einsum(
        "nchd,nhde->nche", key_blocks, suffix_states, preferred_element_type=jnp.float32
    )
    grad_value = grad_value + jnp.einsum(
        "nhct,nche->nthe", weights, grad_blocks, preferred_element_type=jnp.float32
    )
    out_shape = (1, tokens, features)
    return (
        attended,
        grad_query.reshape(out_shape).astype(jnp.bfloat16),
        grad_key.reshape(out_shape).astype(jnp.bfloat16),
        grad_value.reshape(out_shape).astype(jnp.bfloat16),
        grad_gain,
    )


def solution(mesh):
    placed = (
        P("dp", "seq", None),
        P("dp", "seq", None),
        P("dp", "seq", None),
        P(),
        P("dp", "seq", None),
    )
    return jax.shard_map(
        local_body,
        mesh=mesh,
        in_specs=placed,
        out_specs=(
            P("dp", "seq", None),
            P("dp", "seq", None),
            P("dp", "seq", None),
            P("dp", "seq", None),
            P(),
        ),
        check_vma=False,
    )
```

```python
import jax
import jax.numpy as jnp
from jax import lax
from jax.sharding import PartitionSpec as P

HEADS = 12
HEAD_DIM = 128
BLOCK = 256


norm_eps = 1e-05


def carried_in(value, axis, backward, after=None):
    count = lax.axis_size(axis)
    lanes = value.shape[-1]
    rows = value.reshape(count, -1, lanes)
    parts = lax.all_to_all(rows, axis, 0, 0)
    row = lax.broadcasted_iota(jnp.int32, (count, count), 0)
    col = lax.broadcasted_iota(jnp.int32, (count, count), 1)
    strict = ((row < col) if backward else (row > col)).astype(jnp.float32)
    if after is not None:
        strict = strict + 0.0 * after
    shifted = jnp.einsum(
        "ij,jkl->ikl",
        strict,
        parts,
        precision=lax.Precision.HIGHEST,
        preferred_element_type=jnp.float32,
    )
    back = lax.all_to_all(shifted, axis, 0, 0)
    return back.reshape(value.shape)


def butterfly_sum(value, axis):
    count = lax.axis_size(axis)
    step = 1
    while step < count:
        radix = 4 if step * 4 <= count else 2
        got = [
            lax.ppermute(value, axis, [(i, i ^ (k * step)) for i in range(count)])
            for k in range(1, radix)
        ]
        if radix == 4:
            value = (value + got[0]) + (got[1] + got[2])
        else:
            value = value + got[0]
        step *= radix
    return value


def lower_mask(length):
    row_index = lax.broadcasted_iota(jnp.int32, (length, length), 0)
    col_index = lax.broadcasted_iota(jnp.int32, (length, length), 1)
    return row_index >= col_index


def local_body(query_rows, key_rows, value_rows, norm_gain, grad_output):
    tokens = query_rows.shape[1]
    features = query_rows.shape[2]
    blocks = tokens // BLOCK
    block_shape = (blocks, BLOCK, HEADS, HEAD_DIM)
    queries = query_rows.reshape(block_shape)
    key_blocks = key_rows.reshape(block_shape)
    value_blocks = value_rows.reshape(block_shape)
    causal = lower_mask(BLOCK)
    local_states = jnp.einsum(
        "nchd,nche->nhde", key_blocks, value_blocks, preferred_element_type=jnp.float32
    )
    device_total = jnp.sum(local_states, axis=0)
    carried = carried_in(device_total, "seq", False)
    running = jnp.cumsum(local_states, axis=0)
    before = jnp.concatenate([local_states[:1] * 0.0, running[:-1]], axis=0)
    states = (carried[None] + before).astype(jnp.bfloat16)
    scores = jnp.einsum("nchd,nthd->nhct", queries, key_blocks, preferred_element_type=jnp.float32)
    weights = jnp.where(causal, scores, 0.0).astype(jnp.bfloat16)
    combined = jnp.einsum("nchd,nhde->nche", queries, states, preferred_element_type=jnp.float32)
    combined = combined + jnp.einsum(
        "nhct,nthe->nche", weights, value_blocks, preferred_element_type=jnp.float32
    )
    combined = combined.reshape(1, tokens, features)
    inverse = lax.rsqrt(jnp.mean(combined * combined, axis=-1, keepdims=True) + norm_eps)
    normed = combined * inverse
    attended = (normed * norm_gain).astype(jnp.bfloat16)
    upstream = grad_output.astype(jnp.float32)
    gain_terms = jnp.sum(upstream * normed, axis=(0, 1))
    grad_normed = upstream * norm_gain
    grad_combined = inverse * (
        grad_normed - normed * jnp.mean(grad_normed * normed, axis=-1, keepdims=True)
    )
    grad_blocks = grad_combined.astype(jnp.bfloat16).reshape(block_shape)
    query_parts = jnp.einsum(
        "nchd,nche->nhde", queries, grad_blocks, preferred_element_type=jnp.float32
    )
    gain_dp = butterfly_sum(gain_terms, "dp")
    suffix = carried_in(jnp.sum(query_parts, axis=0), "seq", True, gain_dp[0])
    grad_gain = butterfly_sum(gain_dp, "seq")
    from_end = lax.cumsum(query_parts, axis=0, reverse=True)
    behind = jnp.concatenate([from_end[1:], query_parts[-1:] * 0.0], axis=0)
    suffix_states = (suffix[None] + behind).astype(jnp.bfloat16)
    grad_scores = jnp.einsum(
        "nche,nthe->nhct", grad_blocks, value_blocks, preferred_element_type=jnp.float32
    )
    grad_weights = jnp.where(causal, grad_scores, 0.0).astype(jnp.bfloat16)
    grad_query = jnp.einsum(
        "nche,nhde->nchd", grad_blocks, states, preferred_element_type=jnp.float32
    )
    grad_query = grad_query + jnp.einsum(
        "nhct,nthd->nchd", grad_weights, key_blocks, preferred_element_type=jnp.float32
    )
    key_local = jnp.einsum(
        "nhct,nchd->nthd", grad_weights, queries, preferred_element_type=jnp.float32
    )
    value_local = jnp.einsum(
        "nhct,nche->nthe", weights, grad_blocks, preferred_element_type=jnp.float32
    )
    grad_key = jnp.einsum(
        "nche,nhde->nchd", value_blocks, suffix_states, preferred_element_type=jnp.float32
    )
    grad_key = grad_key + key_local
    grad_value = jnp.einsum(
        "nchd,nhde->nche", key_blocks, suffix_states, preferred_element_type=jnp.float32
    )
    grad_value = grad_value + value_local
    out_shape = (1, tokens, features)
    return (
        attended,
        grad_query.reshape(out_shape).astype(jnp.bfloat16),
        grad_key.reshape(out_shape).astype(jnp.bfloat16),
        grad_value.reshape(out_shape).astype(jnp.bfloat16),
        grad_gain,
    )


def solution(mesh):
    placed = (
        P("dp", "seq", None),
        P("dp", "seq", None),
        P("dp", "seq", None),
        P(),
        P("dp", "seq", None),
    )
    return jax.shard_map(
        local_body,
        mesh=mesh,
        in_specs=placed,
        out_specs=(
            P("dp", "seq", None),
            P("dp", "seq", None),
            P("dp", "seq", None),
            P("dp", "seq", None),
            P(),
        ),
        check_vma=False,
    )
```

```python
import jax
import jax.numpy as jnp
from jax import lax
from jax.sharding import PartitionSpec as P

HEADS = 12
HEAD_DIM = 128
BLOCK = 256


norm_eps = 1e-05


def carried_in(value, axis, backward, after=None):
    count = lax.axis_size(axis)
    lanes = value.shape[-1]
    rows = value.reshape(count, -1, lanes)
    parts = lax.all_to_all(rows, axis, 0, 0)
    row = lax.broadcasted_iota(jnp.int32, (count, count), 0)
    col = lax.broadcasted_iota(jnp.int32, (count, count), 1)
    strict = ((row < col) if backward else (row > col)).astype(jnp.float32)
    if after is not None:
        strict = strict + 0.0 * after
    shifted = jnp.einsum(
        "ij,jkl->ikl",
        strict,
        parts,
        precision=lax.Precision.HIGHEST,
        preferred_element_type=jnp.float32,
    )
    back = lax.all_to_all(shifted, axis, 0, 0)
    return back.reshape(value.shape)


def butterfly_sum(value, axis, rounds=None):
    count = lax.axis_size(axis)
    if rounds is None:
        rounds, step = [], 1
        while step < count:
            rounds.append((step, 4 if step * 4 <= count else 2))
            step *= rounds[-1][1]
    for step, radix in rounds:
        got = [
            lax.ppermute(value, axis, [(i, i ^ (k * step)) for i in range(count)])
            for k in range(1, radix)
        ]
        if radix == 4:
            value = (value + got[0]) + (got[1] + got[2])
        else:
            value = value + got[0]
    return value


def lower_mask(length):
    row_index = lax.broadcasted_iota(jnp.int32, (length, length), 0)
    col_index = lax.broadcasted_iota(jnp.int32, (length, length), 1)
    return row_index >= col_index


def local_body(query_rows, key_rows, value_rows, norm_gain, grad_output):
    tokens = query_rows.shape[1]
    features = query_rows.shape[2]
    blocks = tokens // BLOCK
    block_shape = (blocks, BLOCK, HEADS, HEAD_DIM)
    queries = query_rows.reshape(block_shape)
    key_blocks = key_rows.reshape(block_shape)
    value_blocks = value_rows.reshape(block_shape)
    causal = lower_mask(BLOCK)
    local_states = jnp.einsum(
        "nchd,nche->nhde", key_blocks, value_blocks, preferred_element_type=jnp.float32
    )
    device_total = jnp.sum(local_states, axis=0)
    carried = carried_in(device_total, "seq", False)
    running = jnp.cumsum(local_states, axis=0)
    before = jnp.concatenate([local_states[:1] * 0.0, running[:-1]], axis=0)
    states = (carried[None] + before).astype(jnp.bfloat16)
    scores = jnp.einsum("nchd,nthd->nhct", queries, key_blocks, preferred_element_type=jnp.float32)
    weights = jnp.where(causal, scores, 0.0).astype(jnp.bfloat16)
    combined = jnp.einsum("nchd,nhde->nche", queries, states, preferred_element_type=jnp.float32)
    combined = combined + jnp.einsum(
        "nhct,nthe->nche", weights, value_blocks, preferred_element_type=jnp.float32
    )
    combined = combined.reshape(1, tokens, features)
    inverse = lax.rsqrt(jnp.mean(combined * combined, axis=-1, keepdims=True) + norm_eps)
    normed = combined * inverse
    attended = (normed * norm_gain).astype(jnp.bfloat16)
    upstream = grad_output.astype(jnp.float32)
    gain_terms = jnp.sum(upstream * normed, axis=(0, 1))
    grad_normed = upstream * norm_gain
    grad_combined = inverse * (
        grad_normed - normed * jnp.mean(grad_normed * normed, axis=-1, keepdims=True)
    )
    grad_blocks = grad_combined.astype(jnp.bfloat16).reshape(block_shape)
    query_parts = jnp.einsum(
        "nchd,nche->nhde", queries, grad_blocks, preferred_element_type=jnp.float32
    )
    gain_dp = butterfly_sum(gain_terms, "dp", ((1, 2), (2, 4)))
    suffix = carried_in(jnp.sum(query_parts, axis=0), "seq", True, gain_dp[0])
    grad_gain = butterfly_sum(gain_dp, "seq")
    from_end = lax.cumsum(query_parts, axis=0, reverse=True)
    behind = jnp.concatenate([from_end[1:], query_parts[-1:] * 0.0], axis=0)
    suffix_states = (suffix[None] + behind).astype(jnp.bfloat16)
    grad_scores = jnp.einsum(
        "nche,nthe->nhct", grad_blocks, value_blocks, preferred_element_type=jnp.float32
    )
    grad_weights = jnp.where(causal, grad_scores, 0.0).astype(jnp.bfloat16)
    grad_query = jnp.einsum(
        "nche,nhde->nchd", grad_blocks, states, preferred_element_type=jnp.float32
    )
    grad_query = grad_query + jnp.einsum(
        "nhct,nthd->nchd", grad_weights, key_blocks, preferred_element_type=jnp.float32
    )
    grad_key = jnp.einsum(
        "nche,nhde->nchd", value_blocks, suffix_states, preferred_element_type=jnp.float32
    )
    grad_key = grad_key + jnp.einsum(
        "nhct,nchd->nthd", grad_weights, queries, preferred_element_type=jnp.float32
    )
    grad_value = jnp.einsum(
        "nchd,nhde->nche", key_blocks, suffix_states, preferred_element_type=jnp.float32
    )
    grad_value = grad_value + jnp.einsum(
        "nhct,nche->nthe", weights, grad_blocks, preferred_element_type=jnp.float32
    )
    out_shape = (1, tokens, features)
    return (
        attended,
        grad_query.reshape(out_shape).astype(jnp.bfloat16),
        grad_key.reshape(out_shape).astype(jnp.bfloat16),
        grad_value.reshape(out_shape).astype(jnp.bfloat16),
        grad_gain,
    )


def solution(mesh):
    placed = (
        P("dp", "seq", None),
        P("dp", "seq", None),
        P("dp", "seq", None),
        P(),
        P("dp", "seq", None),
    )
    return jax.shard_map(
        local_body,
        mesh=mesh,
        in_specs=placed,
        out_specs=(
            P("dp", "seq", None),
            P("dp", "seq", None),
            P("dp", "seq", None),
            P("dp", "seq", None),
            P(),
        ),
        check_vma=False,
    )
```

```python
import jax
import jax.numpy as jnp
from jax import lax
from jax.sharding import PartitionSpec as P

HEADS = 12
HEAD_DIM = 128
BLOCK = 256


norm_eps = 1e-05


def carried_in(value, axis, backward, after=None):
    count = lax.axis_size(axis)
    lanes = value.shape[-1]
    rows = value.reshape(count, -1, lanes)
    parts = lax.all_to_all(rows, axis, 0, 0)
    row = lax.broadcasted_iota(jnp.int32, (count, count), 0)
    col = lax.broadcasted_iota(jnp.int32, (count, count), 1)
    strict = ((row < col) if backward else (row > col)).astype(jnp.float32)
    if after is not None:
        strict = strict + 0.0 * after
    shifted = jnp.einsum(
        "ij,jkl->ikl",
        strict,
        parts,
        precision=lax.Precision.HIGHEST,
        preferred_element_type=jnp.float32,
    )
    back = lax.all_to_all(shifted, axis, 0, 0)
    return back.reshape(value.shape)


def butterfly_sum(value, axis):
    count = lax.axis_size(axis)
    step = 1
    while step < count:
        radix = 4 if step * 4 <= count else 2
        got = [
            lax.ppermute(value, axis, [(i, i ^ (k * step)) for i in range(count)])
            for k in range(1, radix)
        ]
        if radix == 4:
            value = (value + got[0]) + (got[1] + got[2])
        else:
            value = value + got[0]
        step *= radix
    return value


def lower_mask(length):
    row_index = lax.broadcasted_iota(jnp.int32, (length, length), 0)
    col_index = lax.broadcasted_iota(jnp.int32, (length, length), 1)
    return row_index >= col_index


def local_body(query_rows, key_rows, value_rows, norm_gain, grad_output):
    tokens = query_rows.shape[1]
    features = query_rows.shape[2]
    blocks = tokens // BLOCK
    block_shape = (blocks, BLOCK, HEADS, HEAD_DIM)
    queries = query_rows.reshape(block_shape)
    key_blocks = key_rows.reshape(block_shape)
    value_blocks = value_rows.reshape(block_shape)
    causal = lower_mask(BLOCK)
    local_states = jnp.einsum(
        "nchd,nche->nhde", key_blocks, value_blocks, preferred_element_type=jnp.float32
    )
    device_total = jnp.sum(local_states, axis=0)
    carried = carried_in(device_total, "seq", False)
    running = jnp.cumsum(local_states, axis=0)
    before = jnp.concatenate([local_states[:1] * 0.0, running[:-1]], axis=0)
    states = (carried[None] + before).astype(jnp.bfloat16)
    scores = jnp.einsum("nchd,nthd->nhct", queries, key_blocks, preferred_element_type=jnp.float32)
    weights = jnp.where(causal, scores, 0.0).astype(jnp.bfloat16)
    combined = jnp.einsum("nchd,nhde->nche", queries, states, preferred_element_type=jnp.float32)
    combined = combined + jnp.einsum(
        "nhct,nthe->nche", weights, value_blocks, preferred_element_type=jnp.float32
    )
    combined = combined.reshape(1, tokens, features)
    inverse = lax.rsqrt(jnp.mean(combined * combined, axis=-1, keepdims=True) + norm_eps)
    normed = combined * inverse
    attended = (normed * norm_gain).astype(jnp.bfloat16)
    upstream = grad_output.astype(jnp.float32)
    gain_terms = jnp.sum(upstream * normed, axis=(0, 1))
    grad_normed = upstream * norm_gain
    grad_combined = inverse * (
        grad_normed - normed * jnp.mean(grad_normed * normed, axis=-1, keepdims=True)
    )
    grad_blocks = grad_combined.astype(jnp.bfloat16).reshape(block_shape)
    query_parts = jnp.einsum(
        "nchd,nche->nhde", queries, grad_blocks, preferred_element_type=jnp.float32
    )
    gain_dp = butterfly_sum(gain_terms, "dp")
    suffix = carried_in(jnp.sum(query_parts, axis=0), "seq", True, gain_dp[0])
    grad_gain = butterfly_sum(gain_dp, "seq")
    from_end = lax.cumsum(query_parts, axis=0, reverse=True)
    behind = jnp.concatenate([from_end[1:], query_parts[-1:] * 0.0], axis=0)
    suffix_states = (suffix[None] + behind).astype(jnp.bfloat16)
    grad_scores = jnp.einsum(
        "nche,nthe->nhct", grad_blocks, value_blocks, preferred_element_type=jnp.float32
    )
    grad_weights = jnp.where(causal, grad_scores, 0.0).astype(jnp.bfloat16)
    grad_query = jnp.einsum(
        "nche,nhde->nchd", grad_blocks, states, preferred_element_type=jnp.float32
    )
    grad_query = grad_query + jnp.einsum(
        "nhct,nthd->nchd", grad_weights, key_blocks, preferred_element_type=jnp.float32
    )
    grad_key = jnp.einsum(
        "nche,nhde->nchd", value_blocks, suffix_states, preferred_element_type=jnp.float32
    )
    grad_key = grad_key + jnp.einsum(
        "nhct,nchd->nthd", grad_weights, queries, preferred_element_type=jnp.float32
    )
    grad_value = jnp.einsum(
        "nchd,nhde->nche", key_blocks, suffix_states, preferred_element_type=jnp.float32
    )
    grad_value = grad_value + jnp.einsum(
        "nhct,nche->nthe", weights, grad_blocks, preferred_element_type=jnp.float32
    )
    out_shape = (1, tokens, features)
    return (
        attended,
        grad_query.reshape(out_shape).astype(jnp.bfloat16),
        grad_key.reshape(out_shape).astype(jnp.bfloat16),
        grad_value.reshape(out_shape).astype(jnp.bfloat16),
        grad_gain,
    )


def solution(mesh):
    placed = (
        P("dp", "seq", None),
        P("dp", "seq", None),
        P("dp", "seq", None),
        P(),
        P("dp", "seq", None),
    )
    return (jax.shard_map(
        local_body,
        mesh=mesh,
        in_specs=placed,
        out_specs=(
            P("dp", "seq", None),
            P("dp", "seq", None),
            P("dp", "seq", None),
            P("dp", "seq", None),
            P(),
        ),
        check_vma=False,
    ))
```
